32 devices in a mesh: pair: 8 (over y, x, core), ints: 4 (over z).
Axes of the slice: x: 2, y: 2, z: 4, core: 2. Of those that a mesh axis runs over, the one named last changes fastest.
Arguments:
- t_amps: bfloat16 [32, 8, 4096], P('pair', None, 'ints'), may hold values from -6 to 6
- block_mask: int32 [32, 8, 64], P('pair', None, 'ints'), may hold values 0 or 1
- factors: bfloat16 [8, 64, 64, 128], P('pair', 'ints'), may hold values from -0.75 to 0.75
- links: int32 [8, 64, 32], P('pair', 'ints'), may hold values from 0 to 63, as said below
- link_counts: int32 [8, 64], P('pair', 'ints'), may hold values from 8 to 32, as said below
Outputs:
- ladder: bfloat16 [32, 8, 4096], P('pair', None, 'ints')
The draws below stay inside these ranges and needn't reach their ends.
Inputs may be any that keep to these rules, and one draw needn't show every extreme that they name: `links`: the 32 slots of a tile name distinct tiles of its own block; only the first link_counts slots are used. `link_counts`: in every block, tile 0 uses all 32 slots.
All inputs are finite; a program needn't handle non-finite values. No bound on the sum of `block_mask` on one device may be relied on, other than what follows from the above.
Results may differ from the reference program's by a relative error of at most 0.008.
Values may be sent and summed in bfloat16 or wider, within the bound.
A program may use at most 128 MiB of HBM per device.

```python
import jax
import jax.numpy as jnp
from jax import lax

TILE = 64
NCHOL = 128
NBLK = 8
GT = 64
NB = 32
PAIRS = 32


def draw_links(key, part):
    scores = jax.random.randint(jax.random.fold_in(key, 11), (NBLK, GT, GT), 0, 4096)
    scores = scores * GT + jnp.arange(GT, dtype=jnp.int32)[None, None, :]
    order = jnp.argsort(scores, axis=-1, stable=True).astype(jnp.int32)
    return order[:, :, :NB]


def draw_link_counts(key, part):
    counts = jax.random.randint(jax.random.fold_in(key, 23), (NBLK, GT), max(1, NB // 4), NB + 1)
    return counts.at[:, 0].set(NB).astype(jnp.int32)


def set_ends(values, own_key, low, top_value):
    index_at = [jax.random.randint(jax.random.fold_in(own_key, axis), (), 0, length) for axis, length in enumerate(values.shape)]
    widest = values.shape.index(max(values.shape))
    neighbour = index_at[:widest] + [(index_at[widest] + 1) % values.shape[widest]] + index_at[widest + 1:]
    return values.at[tuple(index_at)].set(low).at[tuple(neighbour)].set(top_value)


def level_of(stream_key, dims, split, smallest, high):
    def one(dim, shards_of):
        steps = jax.random.uniform(jax.random.fold_in(jax.random.fold_in(stream_key, 6), dim), (shards_of,), jnp.float32, smallest / len(split), high / len(split))
        return jnp.repeat(jnp.exp(steps), dims[dim] // shards_of).reshape((-1,) + (1,) * (len(dims) - dim - 1))

    loudness = one(*split[0])
    for cut in split[1:]:
        loudness = loudness * one(*cut)
    return loudness


def centred(own_key, shape, scale, bound, pieces=(), held_as=jnp.bfloat16):
    loudness = level_of(own_key, shape, pieces, -0.22, 0.18) if pieces else 1.0
    values = jax.random.normal(own_key, shape, jnp.float32) * scale * loudness
    return jnp.minimum(jnp.maximum(values, -bound), bound).astype(held_as)


def setup_inputs(seed: int = 0) -> dict:
    arg_keys = jax.random.split(jax.random.key(seed), 6)
    t_amps = centred(arg_keys[0], (PAIRS, NBLK, GT * TILE), 1.0, 6.0, ((0, 8), (2, 4)))
    block_mask = set_ends((jax.random.randint(arg_keys[1], (PAIRS, NBLK, GT), 0, 4) < 3).astype(jnp.int32), jax.random.fold_in(arg_keys[1], 1), 0, 1)
    factors = centred(arg_keys[2], (NBLK, GT, TILE, NCHOL), (1.2 * (NCHOL * NB * TILE) ** -0.25), 0.75, ((0, 8), (1, 4)))
    links = draw_links(jax.random.fold_in(arg_keys[5], 71), 0)
    link_counts = draw_link_counts(jax.random.fold_in(arg_keys[5], 71), 0)
    return {"t_amps": t_amps, "block_mask": block_mask, "factors": factors, "links": links, "link_counts": link_counts}


def reference(t_amps, block_mask, factors, links, link_counts):
    amps4 = t_amps.astype(jnp.float32).reshape(PAIRS, NBLK, GT, TILE)
    masked = amps4 * block_mask[:, :, :, None].astype(jnp.float32)
    masked = jnp.transpose(masked, (1, 0, 2, 3))
    slots = jnp.arange(NB, dtype=jnp.int32)
    tiles = jnp.arange(GT, dtype=jnp.int32)

    def one_block(inputs):
        amps, fac, idx, cnt = inputs
        fac_wide = fac.astype(jnp.float32)
        prods = jnp.einsum("syq,psy->sqp", fac_wide, amps, precision=lax.Precision.HIGHEST)
        used = (slots[None, :] < cnt[:, None]).astype(jnp.float32)
        lmat = jnp.sum((idx[:, :, None] == tiles[None, None, :]).astype(jnp.float32) * used[:, :, None], axis=1)
        summed = jnp.dot(lmat, prods.reshape(GT, NCHOL * PAIRS), precision=lax.Precision.HIGHEST)
        summed = summed.reshape(GT, NCHOL, PAIRS)
        return jnp.einsum("rxq,rqp->rxp", fac_wide, summed, precision=lax.Precision.HIGHEST)

    result = lax.map(one_block, (masked, factors, links, link_counts))
    result = jnp.transpose(result, (3, 0, 1, 2)).reshape(PAIRS, NBLK, GT * TILE)
    return result.astype(jnp.bfloat16)
```

```python
import functools

import jax
import jax.numpy as jnp
from jax import lax
from jax.experimental import pallas as pl
from jax.experimental.pallas import tpu as pltpu
from jax.sharding import PartitionSpec as P

ROWS = 8
DEPTH = 256


def iota(shape, dim):
    return lax.broadcasted_iota(jnp.int32, shape, dim)


def dot(a, b):
    return jnp.dot(a, b, preferred_element_type=jnp.float32)


def ones_where(cond):
    return jnp.where(cond, 1.0, 0.0).astype(jnp.bfloat16)


def kernel(
    np_, nz, t_hbm, m_hbm, f_hbm, l_hbm, c_hbm, o_ref,
    t_v, m_v, f_v, l_v, c_v, stage1, recv1, g_buf, li, stage2, recv2,
    in_sem, s1, r1, sg, rg, s2, r2,
):
    me = lax.axis_index("pair")
    mz = lax.axis_index("ints")
    pd, nb, width = t_v.shape
    tc, tile, nq = f_v.shape[1:]
    gt = nz * tc
    parts = ROWS // pd
    wh = width // parts
    nc = np_ * pd // ROWS
    gs = DEPTH // tile
    ng = tc // gs
    bf, f32 = jnp.bfloat16, jnp.float32

    loads = [
        pltpu.make_async_copy(src, dst, in_sem.at[i])
        for i, (src, dst) in enumerate(
            ((t_hbm, t_v), (m_hbm, m_v), (l_hbm, l_v), (c_hbm, c_v), (f_hbm, f_v))
        )
    ]
    for load in loads:
        load.start()

    barrier = pltpu.get_barrier_semaphore()
    for rel in range(1, np_):
        pl.semaphore_signal(
            barrier, inc=1, device_id={"pair": lax.rem(me + rel, np_)},
            device_id_type=pl.DeviceIdType.MESH,
        )
    has_left, has_right = mz > 0, mz < nz - 1

    @pl.when(has_left)
    def _():
        pl.semaphore_signal(
            barrier, inc=1, device_id={"ints": mz - 1}, device_id_type=pl.DeviceIdType.MESH
        )

    @pl.when(has_right)
    def _():
        pl.semaphore_signal(
            barrier, inc=1, device_id={"ints": mz + 1}, device_id_type=pl.DeviceIdType.MESH
        )

    loads[0].wait()
    loads[1].wait()
    spread = ones_where(
        (iota((tc, width), 1) >= iota((tc, width), 0) * tile)
        & (iota((tc, width), 1) < iota((tc, width), 0) * tile + tile)
    )
    amps = t_v[...].astype(f32).reshape(pd * nb, width)
    mask = m_v[...].astype(f32).reshape(pd * nb, tc).astype(bf)
    masked = (amps * dot(mask, spread)).astype(bf)
    piled = jnp.concatenate([masked[:, h * wh:(h + 1) * wh] for h in range(parts)], axis=0)
    shape = (nb * ROWS, ROWS * nb)
    row, col = iota(shape, 0), iota(shape, 1)
    order = ones_where(col == (row & (ROWS - 1)) * nb + lax.shift_right_logical(row, 3))
    slabs = dot(order, piled).reshape(nb, ROWS, wh).astype(bf)
    stage1[...] = slabs
    recv1[me] = stage1[me]

    to_wait = np_ - 1 + jnp.where(has_left, 1, 0) + jnp.where(has_right, 1, 0)
    pl.semaphore_wait(barrier, to_wait)

    def swap(stage, recv, ssem, rsem, peer, slot):
        return pltpu.make_async_remote_copy(
            src_ref=stage.at[peer], dst_ref=recv.at[slot],
            send_sem=ssem.at[peer], recv_sem=rsem.at[slot],
            device_id={"pair": peer}, device_id_type=pl.DeviceIdType.MESH,
        )

    for rel in range(1, np_):
        peer = lax.rem(me + rel, np_)
        swap(stage1, recv1, s1, r1, peer, me).start()

    loads[2].wait()
    loads[3].wait()
    links = l_v[0]
    eye = iota((tc, tc), 0) == iota((tc, tc), 1)
    counts = jnp.sum(
        jnp.where(eye, jnp.broadcast_to(c_v[...], (tc, tc)), 0), axis=1, keepdims=True
    )
    links = jnp.where(iota(links.shape, 1) < counts, links, -1)
    tiles = iota((tc, gt), 1)
    hits = jnp.zeros((tc, gt), f32)
    for k in range(links.shape[1]):
        hits = hits + jnp.where(links[:, k:k + 1] == tiles, 1.0, 0.0)
    rep = ones_where(
        lax.shift_right_logical(iota((tc * ROWS, tc), 0), 3) == iota((tc * ROWS, tc), 1)
    )
    tall = dot(rep, hits.astype(bf)).astype(bf)
    wide = (gt, gt * ROWS)
    across = ones_where(iota(wide, 0) == lax.shift_right_logical(iota(wide, 1), 3))
    full = (tc * ROWS, gt * ROWS)
    same = (iota(full, 0) & (ROWS - 1)) == (iota(full, 1) & (ROWS - 1))
    li[...] = jnp.where(same, dot(tall, across), 0.0).astype(bf)
    loads[4].wait()

    def hop(src, c, side):
        target = mz + 1 if side else mz - 1
        return pltpu.make_async_remote_copy(
            src_ref=g_buf.at[src, c], dst_ref=g_buf.at[src, c],
            send_sem=sg.at[side, src, c], recv_sem=rg.at[src, c],
            device_id={"ints": target}, device_id_type=pl.DeviceIdType.MESH,
        )

    lane_tile = lax.shift_right_logical(iota((ROWS, DEPTH), 1), tile.bit_length() - 1)
    sub = iota((ROWS, wh), 0)

    def chunk_of(i):
        return lax.rem(lax.div(me, parts) + i, nc)

    def shifted(x, by):
        by = by % ROWS
        return x if by == 0 else pltpu.roll(x, by, 0)

    def rows_of(pieces):
        out = pieces[0]
        for j in range(1, parts):
            out = jnp.where(sub >= j * pd, pieces[j], out)
        return out

    for i in range(nc):
        c = chunk_of(i)
        got = []
        for d in range(parts):
            dev = c * parts + d

            @pl.when(dev != me)
            def _(dev=dev):
                swap(stage1, recv1, s1, r1, dev, dev).wait_recv()

            got.append(dev)
        got = [recv1[dev].astype(f32) for dev in got]
        blocks = []
        for h in range(parts):
            part = rows_of([shifted(got[d], (d - h) * pd) for d in range(parts)])
            for j in range(wh // DEPTH):
                group = part[:, j * DEPTH:(j + 1) * DEPTH]
                lhs = jnp.concatenate(
                    [jnp.where(lane_tile == k, group, 0.0) for k in range(gs)], axis=0
                ).astype(bf)
                g = h * (wh // DEPTH) + j
                near = f_v[0, g * gs:(g + 1) * gs].reshape(DEPTH, nq)
                blocks.append(dot(lhs, near).astype(bf))
        g_buf[mz, c] = jnp.concatenate(blocks, axis=0)

        @pl.when(has_right)
        def _(c=c):
            hop(mz, c, 1).start()

        @pl.when(has_left)
        def _(c=c):
            hop(mz, c, 0).start()

    def take(dist, i, forward):
        c = chunk_of(i)

        @pl.when(mz - dist >= 0)
        def _():
            hop(mz - dist, c, 1).wait_recv()
            if forward:
                @pl.when(has_right)
                def _():
                    hop(mz - dist, c, 1).start()

        @pl.when(mz + dist < nz)
        def _():
            hop(mz + dist, c, 0).wait_recv()
            if forward:
                @pl.when(has_left)
                def _():
                    hop(mz + dist, c, 0).start()

    for dist in range(1, nz - 1):
        for i in range(nc):
            take(dist, i, True)

    for i in range(nc):
        c = chunk_of(i)
        if nz > 1:
            take(nz - 1, i, False)
        every = g_buf[:, c].reshape(gt * ROWS, nq)
        total = dot(li[...], every).astype(bf)
        flat = []
        for g in range(ng):
            near = f_v[0, g * gs:(g + 1) * gs].reshape(DEPTH, nq)
            mine = total[g * gs * ROWS:(g + 1) * gs * ROWS]
            crossed = lax.dot_general(
                mine, near, (((1,), (1,)), ((), ())), preferred_element_type=f32
            )
            kept = crossed[:ROWS]
            for k in range(1, gs):
                kept = jnp.where(lane_tile == k, crossed[k * ROWS:(k + 1) * ROWS], kept)
            flat.append(kept)
        flat = jnp.concatenate(flat, axis=1)
        halves = [flat[:, h * wh:(h + 1) * wh] for h in range(parts)]
        for d in range(parts):
            dev = c * parts + d
            slab = rows_of([shifted(halves[h], (h - d) * pd) for h in range(parts)])
            stage2[dev] = slab.astype(bf)

            @pl.when(dev != me)
            def _(dev=dev):
                swap(stage2, recv2, s2, r2, dev, me).start()

            @pl.when(dev == me)
            def _(dev=dev):
                recv2[dev] = stage2[dev]

    for rel in range(1, np_):
        peer = lax.rem(me + rel, np_)
        swap(stage2, recv2, s2, r2, peer, peer).wait_recv()
    landed = recv2[...].astype(f32).reshape(nb * ROWS, wh).astype(bf)
    shape = (pd * nb, nb * ROWS)
    row, col = iota(shape, 0), iota(shape, 1)
    for h in range(parts):
        back = ones_where(
            ((col & (ROWS - 1)) - h * pd) * nb + lax.shift_right_logical(col, 3) == row
        )
        o_ref[:, :, h * wh:(h + 1) * wh] = dot(back, landed).reshape(pd, nb, wh).astype(bf)

    for rel in range(1, np_):
        peer = lax.rem(me + rel, np_)
        swap(stage1, recv1, s1, r1, peer, me).wait_send()
        swap(stage2, recv2, s2, r2, peer, me).wait_send()
    for i in range(nc):
        for dist in range(nz - 1):
            @pl.when(has_right & (mz - dist >= 0))
            def _(i=i, dist=dist):
                hop(mz - dist, chunk_of(i), 1).wait_send()

            @pl.when(has_left & (mz + dist < nz))
            def _(i=i, dist=dist):
                hop(mz + dist, chunk_of(i), 0).wait_send()


def solution(mesh):
    np_, nz = mesh.shape["pair"], mesh.shape["ints"]

    def body(t_amps, block_mask, factors, links, link_counts):
        pd, nb, width = t_amps.shape
        _, tc, tile, nq = factors.shape
        parts = ROWS // pd
        nc = np_ * pd // ROWS
        slabs = (nb, ROWS, width // parts)
        bf = jnp.bfloat16
        return pl.pallas_call(
            functools.partial(kernel, np_, nz),
            out_shape=jax.ShapeDtypeStruct(t_amps.shape, bf),
            in_specs=[pl.BlockSpec(memory_space=pl.ANY)] * 5,
            out_specs=pl.BlockSpec(memory_space=pltpu.VMEM),
            scratch_shapes=[
                pltpu.VMEM(t_amps.shape, bf),
                pltpu.VMEM(block_mask.shape, jnp.int32),
                pltpu.VMEM(factors.shape, bf),
                pltpu.VMEM(links.shape, jnp.int32),
                pltpu.VMEM(link_counts.shape, jnp.int32),
                pltpu.VMEM(slabs, bf),
                pltpu.VMEM(slabs, bf),
                pltpu.VMEM((nz, nc, tc * ROWS, nq), bf),
                pltpu.VMEM((tc * ROWS, nz * tc * ROWS), bf),
                pltpu.VMEM(slabs, bf),
                pltpu.VMEM(slabs, bf),
                pltpu.SemaphoreType.DMA((5,)),
                pltpu.SemaphoreType.DMA((np_,)),
                pltpu.SemaphoreType.DMA((np_,)),
                pltpu.SemaphoreType.DMA((2, nz, nc)),
                pltpu.SemaphoreType.DMA((nz, nc)),
                pltpu.SemaphoreType.DMA((np_,)),
                pltpu.SemaphoreType.DMA((np_,)),
            ],
            compiler_params=pltpu.CompilerParams(collective_id=0, has_side_effects=True),
        )(t_amps, block_mask, factors, links, link_counts)

    placed = (
        P("pair", None, "ints"),
        P("pair", None, "ints"),
        P("pair", "ints", None, None),
        P("pair", "ints", None),
        P("pair", "ints"),
    )
    return jax.shard_map(
        body, mesh=mesh, in_specs=placed, out_specs=P("pair", None, "ints"), check_vma=False
    )
```

```python
import functools

import jax
import jax.numpy as jnp
from jax import lax
from jax.experimental import pallas as pl
from jax.experimental.pallas import tpu as pltpu
from jax.sharding import PartitionSpec as P

ROWS = 8
DEPTH = 256


def iota(shape, dim):
    return lax.broadcasted_iota(jnp.int32, shape, dim)


def dot(a, b):
    return jnp.dot(a, b, preferred_element_type=jnp.float32)


def ones_where(cond):
    return jnp.where(cond, 1.0, 0.0).astype(jnp.bfloat16)


def kernel(
    np_, nz, t_hbm, m_hbm, f_hbm, l_hbm, c_hbm, o_ref,
    t_v, m_v, f_v, l_v, c_v, stage1, recv1, g_buf, li, stage2, recv2,
    l_end, c_end, li_end, p_out, p_in, tot, in_sem, s1, r1, sg, rg, s2, r2, se, re, sp, rp,
):
    me = lax.axis_index("pair")
    mz = lax.axis_index("ints")
    pd, nb, width = t_v.shape
    tc, tile, nq = f_v.shape[1:]
    gt = nz * tc
    parts = ROWS // pd
    wh = width // parts
    nc = np_ * pd // ROWS
    gs = DEPTH // tile
    ng = tc // gs
    bf, f32 = jnp.bfloat16, jnp.float32

    loads = [
        pltpu.make_async_copy(src, dst, in_sem.at[i])
        for i, (src, dst) in enumerate(
            ((t_hbm, t_v), (m_hbm, m_v), (l_hbm, l_v), (c_hbm, c_v), (f_hbm, f_v))
        )
    ]
    for load in loads:
        load.start()

    barrier = pltpu.get_barrier_semaphore()
    for rel in range(1, np_):
        pl.semaphore_signal(
            barrier, inc=1, device_id={"pair": lax.rem(me + rel, np_)},
            device_id_type=pl.DeviceIdType.MESH,
        )
    for rel in range(1, nz):
        pl.semaphore_signal(
            barrier, inc=1, device_id={"ints": lax.rem(mz + rel, nz)},
            device_id_type=pl.DeviceIdType.MESH,
        )

    loads[0].wait()
    loads[1].wait()
    spread = ones_where(
        (iota((tc, width), 1) >= iota((tc, width), 0) * tile)
        & (iota((tc, width), 1) < iota((tc, width), 0) * tile + tile)
    )
    amps = t_v[...].astype(f32).reshape(pd * nb, width)
    mask = m_v[...].astype(f32).reshape(pd * nb, tc).astype(bf)
    masked = (amps * dot(mask, spread)).astype(bf)
    piled = jnp.concatenate([masked[:, h * wh:(h + 1) * wh] for h in range(parts)], axis=0)
    shape = (nb * ROWS, ROWS * nb)
    row, col = iota(shape, 0), iota(shape, 1)
    order = ones_where(col == (row & (ROWS - 1)) * nb + lax.shift_right_logical(row, 3))
    slabs = dot(order, piled).reshape(nb, ROWS, wh).astype(bf)
    stage1[...] = slabs
    recv1[me] = stage1[me]

    pl.semaphore_wait(barrier, np_ + nz - 2)

    def swap(stage, recv, ssem, rsem, peer, slot):
        return pltpu.make_async_remote_copy(
            src_ref=stage.at[peer], dst_ref=recv.at[slot],
            send_sem=ssem.at[peer], recv_sem=rsem.at[slot],
            device_id={"pair": peer}, device_id_type=pl.DeviceIdType.MESH,
        )

    for rel in range(1, np_):
        peer = lax.rem(me + rel, np_)
        swap(stage1, recv1, s1, r1, peer, me).start()

    loads[2].wait()
    loads[3].wait()
    is_end = [mz == 0, mz == nz - 1]
    helps = [mz == 1, mz == nz - 2]

    def tell(side, j):
        src, dst = ((l_v, l_end.at[side]), (c_v, c_end.at[side]))[j]
        return pltpu.make_async_remote_copy(
            src_ref=src, dst_ref=dst, send_sem=se.at[side, j], recv_sem=re.at[side, j],
            device_id={"ints": mz - 1 if side else mz + 1},
            device_id_type=pl.DeviceIdType.MESH,
        )

    for side in range(2):
        @pl.when(is_end[side])
        def _(side=side):
            tell(side, 0).start()
            tell(side, 1).start()

    def spread_links(links, counts):
        eye = iota((tc, tc), 0) == iota((tc, tc), 1)
        counts = jnp.sum(
            jnp.where(eye, jnp.broadcast_to(counts, (tc, tc)), 0), axis=1, keepdims=True
        )
        links = jnp.where(iota(links.shape, 1) < counts, links, -1)
        tiles = iota((tc, gt), 1)
        hits = jnp.zeros((tc, gt), f32)
        for k in range(links.shape[1]):
            hits = hits + jnp.where(links[:, k:k + 1] == tiles, 1.0, 0.0)
        rep = ones_where(
            lax.shift_right_logical(iota((tc * ROWS, tc), 0), 3) == iota((tc * ROWS, tc), 1)
        )
        tall = dot(rep, hits.astype(bf)).astype(bf)
        wide = (gt, gt * ROWS)
        across = ones_where(iota(wide, 0) == lax.shift_right_logical(iota(wide, 1), 3))
        full = (tc * ROWS, gt * ROWS)
        same = (iota(full, 0) & (ROWS - 1)) == (iota(full, 1) & (ROWS - 1))
        return jnp.where(same, dot(tall, across), 0.0).astype(bf)

    li[...] = spread_links(l_v[0], c_v[...])
    for side in range(2):
        @pl.when(helps[side])
        def _(side=side):
            tell(side, 0).wait_recv()
            tell(side, 1).wait_recv()
            li_end[side] = spread_links(l_end[side, 0], c_end[side])

    loads[4].wait()

    def inner(z):
        return (z > 0) & (z < nz - 1)

    def spread_to(target, src, c):
        return pltpu.make_async_remote_copy(
            src_ref=g_buf.at[mz, c], dst_ref=g_buf.at[src, c],
            send_sem=sg.at[target, c], recv_sem=rg.at[src, c],
            device_id={"ints": target}, device_id_type=pl.DeviceIdType.MESH,
        )

    others = [lax.rem(mz + rel, nz) for rel in range(1, nz)]

    def sum_hop(c, side):
        return pltpu.make_async_remote_copy(
            src_ref=p_out.at[side, c], dst_ref=p_in.at[c],
            send_sem=sp.at[side, c], recv_sem=rp.at[c],
            device_id={"ints": mz + 1 if side else mz - 1},
            device_id_type=pl.DeviceIdType.MESH,
        )

    lane_tile = lax.shift_right_logical(iota((ROWS, DEPTH), 1), tile.bit_length() - 1)
    sub = iota((ROWS, wh), 0)

    def chunk_of(i):
        return lax.rem(lax.div(me, parts) + i, nc)

    def shifted(x, by):
        by = by % ROWS
        return x if by == 0 else pltpu.roll(x, by, 0)

    def rows_of(pieces):
        out = pieces[0]
        for j in range(1, parts):
            out = jnp.where(sub >= j * pd, pieces[j], out)
        return out

    for i in range(nc):
        c = chunk_of(i)
        got = []
        for d in range(parts):
            dev = c * parts + d

            @pl.when(dev != me)
            def _(dev=dev):
                swap(stage1, recv1, s1, r1, dev, dev).wait_recv()

            got.append(dev)
        got = [recv1[dev].astype(f32) for dev in got]
        blocks = []
        for h in range(parts):
            part = rows_of([shifted(got[d], (d - h) * pd) for d in range(parts)])
            for j in range(wh // DEPTH):
                group = part[:, j * DEPTH:(j + 1) * DEPTH]
                lhs = jnp.concatenate(
                    [jnp.where(lane_tile == k, group, 0.0) for k in range(gs)], axis=0
                ).astype(bf)
                g = h * (wh // DEPTH) + j
                near = f_v[0, g * gs:(g + 1) * gs].reshape(DEPTH, nq)
                blocks.append(dot(lhs, near).astype(bf))
        g_buf[mz, c] = jnp.concatenate(blocks, axis=0)

        for target in others:
            @pl.when(inner(target))
            def _(target=target, c=c):
                spread_to(target, mz, c).start()

    part_rows = tc * ROWS
    for i in range(nc):
        c = chunk_of(i)

        @pl.when(inner(mz))
        def _(c=c):
            for src in others:
                spread_to(src, src, c).wait_recv()

        for side in range(2):
            @pl.when(helps[side])
            def _(c=c, side=side):
                first, last = (0, nz - 1) if side else (1, nz)
                near = g_buf[first:last, c].reshape((last - first) * part_rows, nq)
                cols = li_end[side, :, first * part_rows:last * part_rows]
                p_out[side, c] = dot(cols, near).astype(bf)
                sum_hop(c, side).start()

        for side in range(2):
            @pl.when(is_end[side])
            def _(c=c, side=side):
                own = (nz - 1) * side
                mine = dot(li[:, own * part_rows:(own + 1) * part_rows], g_buf[own, c])
                sum_hop(c, side).wait_recv()
                tot[...] = mine + p_in[c].astype(f32)

        @pl.when(inner(mz))
        def _(c=c):
            tot[...] = dot(li[...], g_buf[:, c].reshape(gt * ROWS, nq))

        total = tot[...].astype(bf)
        flat = []
        for g in range(ng):
            near = f_v[0, g * gs:(g + 1) * gs].reshape(DEPTH, nq)
            mine = total[g * gs * ROWS:(g + 1) * gs * ROWS]
            crossed = lax.dot_general(
                mine, near, (((1,), (1,)), ((), ())), preferred_element_type=f32
            )
            kept = crossed[:ROWS]
            for k in range(1, gs):
                kept = jnp.where(lane_tile == k, crossed[k * ROWS:(k + 1) * ROWS], kept)
            flat.append(kept)
        flat = jnp.concatenate(flat, axis=1)
        halves = [flat[:, h * wh:(h + 1) * wh] for h in range(parts)]
        for d in range(parts):
            dev = c * parts + d
            slab = rows_of([shifted(halves[h], (h - d) * pd) for h in range(parts)])
            stage2[dev] = slab.astype(bf)

            @pl.when(dev != me)
            def _(dev=dev):
                swap(stage2, recv2, s2, r2, dev, me).start()

            @pl.when(dev == me)
            def _(dev=dev):
                recv2[dev] = stage2[dev]

    for rel in range(1, np_):
        peer = lax.rem(me + rel, np_)
        swap(stage2, recv2, s2, r2, peer, peer).wait_recv()
    landed = recv2[...].astype(f32).reshape(nb * ROWS, wh).astype(bf)
    shape = (pd * nb, nb * ROWS)
    row, col = iota(shape, 0), iota(shape, 1)
    for h in range(parts):
        back = ones_where(
            ((col & (ROWS - 1)) - h * pd) * nb + lax.shift_right_logical(col, 3) == row
        )
        o_ref[:, :, h * wh:(h + 1) * wh] = dot(back, landed).reshape(pd, nb, wh).astype(bf)

    for rel in range(1, np_):
        peer = lax.rem(me + rel, np_)
        swap(stage1, recv1, s1, r1, peer, me).wait_send()
        swap(stage2, recv2, s2, r2, peer, me).wait_send()
    for side in range(2):
        @pl.when(is_end[side])
        def _(side=side):
            tell(side, 0).wait_send()
            tell(side, 1).wait_send()

    for i in range(nc):
        for target in others:
            @pl.when(inner(target))
            def _(target=target, i=i):
                spread_to(target, mz, chunk_of(i)).wait_send()

        for side in range(2):
            @pl.when(helps[side])
            def _(i=i, side=side):
                sum_hop(chunk_of(i), side).wait_send()


def solution(mesh):
    np_, nz = mesh.shape["pair"], mesh.shape["ints"]

    def body(t_amps, block_mask, factors, links, link_counts):
        pd, nb, width = t_amps.shape
        _, tc, tile, nq = factors.shape
        parts = ROWS // pd
        nc = np_ * pd // ROWS
        slabs = (nb, ROWS, width // parts)
        bf = jnp.bfloat16
        return pl.pallas_call(
            functools.partial(kernel, np_, nz),
            out_shape=pltpu.VMEM(t_amps.shape, bf),
            in_specs=[pl.BlockSpec(memory_space=pl.ANY)] * 5,
            out_specs=pl.BlockSpec(memory_space=pltpu.VMEM),
            scratch_shapes=[
                pltpu.VMEM(t_amps.shape, bf),
                pltpu.VMEM(block_mask.shape, jnp.int32),
                pltpu.VMEM(factors.shape, bf),
                pltpu.VMEM(links.shape, jnp.int32),
                pltpu.VMEM(link_counts.shape, jnp.int32),
                pltpu.VMEM(slabs, bf),
                pltpu.VMEM(slabs, bf),
                pltpu.VMEM((nz, nc, tc * ROWS, nq), bf),
                pltpu.VMEM((tc * ROWS, nz * tc * ROWS), bf),
                pltpu.VMEM(slabs, bf),
                pltpu.VMEM(slabs, bf),
                pltpu.VMEM((2,) + links.shape, jnp.int32),
                pltpu.VMEM((2,) + link_counts.shape, jnp.int32),
                pltpu.VMEM((2, tc * ROWS, nz * tc * ROWS), bf),
                pltpu.VMEM((2, nc, tc * ROWS, nq), bf),
                pltpu.VMEM((nc, tc * ROWS, nq), bf),
                pltpu.VMEM((tc * ROWS, nq), jnp.float32),
                pltpu.SemaphoreType.DMA((5,)),
                pltpu.SemaphoreType.DMA((np_,)),
                pltpu.SemaphoreType.DMA((np_,)),
                pltpu.SemaphoreType.DMA((nz, nc)),
                pltpu.SemaphoreType.DMA((nz, nc)),
                pltpu.SemaphoreType.DMA((np_,)),
                pltpu.SemaphoreType.DMA((np_,)),
                pltpu.SemaphoreType.DMA((2, 2)),
                pltpu.SemaphoreType.DMA((2, 2)),
                pltpu.SemaphoreType.DMA((2, nc)),
                pltpu.SemaphoreType.DMA((nc,)),
            ],
            compiler_params=pltpu.CompilerParams(collective_id=0, has_side_effects=True),
        )(t_amps, block_mask, factors, links, link_counts)

    placed = (
        P("pair", None, "ints"),
        P("pair", None, "ints"),
        P("pair", "ints", None, None),
        P("pair", "ints", None),
        P("pair", "ints"),
    )
    return jax.shard_map(
        body, mesh=mesh, in_specs=placed, out_specs=P("pair", None, "ints"), check_vma=False
    )
```

```python
import functools

import jax
import jax.numpy as jnp
from jax import lax
from jax.experimental import pallas as pl
from jax.experimental.pallas import tpu as pltpu
from jax.sharding import PartitionSpec as P

ROWS = 8
DEPTH = 256


def iota(shape, dim):
    return lax.broadcasted_iota(jnp.int32, shape, dim)


def dot(a, b):
    return jnp.dot(a, b, preferred_element_type=jnp.float32)


def ones_where(cond):
    return jnp.where(cond, 1.0, 0.0).astype(jnp.bfloat16)


def kernel(
    np_, nz, t_hbm, m_hbm, f_hbm, l_hbm, c_hbm, o_ref,
    t_v, m_v, f_v, l_v, c_v, stage1, recv1, g_buf, li, stage2, recv2,
    l_end, c_end, li_end, p_out, p_in, tot, in_sem, s1, r1, sg, rg, s2, r2, se, re, sp, rp,
):
    me = lax.axis_index("pair")
    mz = lax.axis_index("ints")
    pd, nb, width = t_v.shape
    tc, tile, nq = f_v.shape[1:]
    gt = nz * tc
    parts = ROWS // pd
    wh = width // parts
    nc = np_ * pd // ROWS
    gs = DEPTH // tile
    ng = tc // gs
    bf, f32 = jnp.bfloat16, jnp.float32

    loads = [
        pltpu.make_async_copy(src, dst, in_sem.at[i])
        for i, (src, dst) in enumerate(
            ((t_hbm, t_v), (m_hbm, m_v), (l_hbm, l_v), (c_hbm, c_v), (f_hbm, f_v))
        )
    ]
    for load in loads:
        load.start()

    barrier = pltpu.get_barrier_semaphore()
    for rel in range(1, np_):
        pl.semaphore_signal(
            barrier, inc=1, device_id={"pair": lax.rem(me + rel, np_)},
            device_id_type=pl.DeviceIdType.MESH,
        )

    def inner(z):
        return (z > 0) & (z < nz - 1)

    def close(a, b):
        return inner(b) | (b == 0) & (a == 1) | (b == nz - 1) & (a == nz - 2)

    others = [lax.rem(mz + rel, nz) for rel in range(1, nz)]
    to_wait = np_ - 1
    for other in others:
        to_wait = to_wait + jnp.where(close(mz, other), 1, 0)

        @pl.when(close(other, mz))
        def _(other=other):
            pl.semaphore_signal(
                barrier, inc=1, device_id={"ints": other},
                device_id_type=pl.DeviceIdType.MESH,
            )

    loads[0].wait()
    loads[1].wait()
    spread = ones_where(
        (iota((tc, width), 1) >= iota((tc, width), 0) * tile)
        & (iota((tc, width), 1) < iota((tc, width), 0) * tile + tile)
    )
    amps = t_v[...].astype(f32).reshape(pd * nb, width)
    mask = m_v[...].astype(f32).reshape(pd * nb, tc).astype(bf)
    masked = (amps * dot(mask, spread)).astype(bf)
    piled = jnp.concatenate([masked[:, h * wh:(h + 1) * wh] for h in range(parts)], axis=0)
    shape = (nb * ROWS, ROWS * nb)
    row, col = iota(shape, 0), iota(shape, 1)
    order = ones_where(col == (row & (ROWS - 1)) * nb + lax.shift_right_logical(row, 3))
    slabs = dot(order, piled).reshape(nb, ROWS, wh).astype(bf)
    stage1[...] = slabs
    recv1[me] = stage1[me]

    pl.semaphore_wait(barrier, to_wait)

    def swap(stage, recv, ssem, rsem, peer, slot):
        return pltpu.make_async_remote_copy(
            src_ref=stage.at[peer], dst_ref=recv.at[slot],
            send_sem=ssem.at[peer], recv_sem=rsem.at[slot],
            device_id={"pair": peer}, device_id_type=pl.DeviceIdType.MESH,
        )

    for rel in range(1, np_):
        peer = lax.rem(me + rel, np_)
        swap(stage1, recv1, s1, r1, peer, me).start()

    loads[2].wait()
    loads[3].wait()
    is_end = [mz == 0, mz == nz - 1]
    helps = [mz == 1, mz == nz - 2]

    def tell(side, j):
        src, dst = ((l_v, l_end.at[side]), (c_v, c_end.at[side]))[j]
        return pltpu.make_async_remote_copy(
            src_ref=src, dst_ref=dst, send_sem=se.at[side, j], recv_sem=re.at[side, j],
            device_id={"ints": mz - 1 if side else mz + 1},
            device_id_type=pl.DeviceIdType.MESH,
        )

    for side in range(2):
        @pl.when(is_end[side])
        def _(side=side):
            tell(side, 0).start()
            tell(side, 1).start()

    def spread_links(links, counts):
        eye = iota((tc, tc), 0) == iota((tc, tc), 1)
        counts = jnp.sum(
            jnp.where(eye, jnp.broadcast_to(counts, (tc, tc)), 0), axis=1, keepdims=True
        )
        links = jnp.where(iota(links.shape, 1) < counts, links, -1)
        tiles = iota((tc, gt), 1)
        hits = jnp.zeros((tc, gt), f32)
        for k in range(links.shape[1]):
            hits = hits + jnp.where(links[:, k:k + 1] == tiles, 1.0, 0.0)
        rep = ones_where(
            lax.shift_right_logical(iota((tc * ROWS, tc), 0), 3) == iota((tc * ROWS, tc), 1)
        )
        tall = dot(rep, hits.astype(bf)).astype(bf)
        wide = (gt, gt * ROWS)
        across = ones_where(iota(wide, 0) == lax.shift_right_logical(iota(wide, 1), 3))
        full = (tc * ROWS, gt * ROWS)
        same = (iota(full, 0) & (ROWS - 1)) == (iota(full, 1) & (ROWS - 1))
        return jnp.where(same, dot(tall, across), 0.0).astype(bf)

    loads[4].wait()

    def spread_to(target, src, c):
        return pltpu.make_async_remote_copy(
            src_ref=g_buf.at[mz, c], dst_ref=g_buf.at[src, c],
            send_sem=sg.at[target, c], recv_sem=rg.at[src, c],
            device_id={"ints": target}, device_id_type=pl.DeviceIdType.MESH,
        )

    def sum_hop(c, side):
        return pltpu.make_async_remote_copy(
            src_ref=p_out.at[side, c], dst_ref=p_in.at[c],
            send_sem=sp.at[side, c], recv_sem=rp.at[c],
            device_id={"ints": mz + 1 if side else mz - 1},
            device_id_type=pl.DeviceIdType.MESH,
        )

    lane_tile = lax.shift_right_logical(iota((ROWS, DEPTH), 1), tile.bit_length() - 1)
    sub = iota((ROWS, wh), 0)

    def chunk_of(i):
        return lax.rem(lax.div(me, parts) + i, nc)

    def shifted(x, by):
        by = by % ROWS
        return x if by == 0 else pltpu.roll(x, by, 0)

    def rows_of(pieces):
        out = pieces[0]
        for j in range(1, parts):
            out = jnp.where(sub >= j * pd, pieces[j], out)
        return out

    for i in range(nc):
        c = chunk_of(i)
        got = []
        for d in range(parts):
            dev = c * parts + d

            @pl.when(dev != me)
            def _(dev=dev):
                swap(stage1, recv1, s1, r1, dev, dev).wait_recv()

            got.append(dev)
        got = [recv1[dev].astype(f32) for dev in got]
        blocks = []
        for h in range(parts):
            part = rows_of([shifted(got[d], (d - h) * pd) for d in range(parts)])
            for j in range(wh // DEPTH):
                group = part[:, j * DEPTH:(j + 1) * DEPTH]
                lhs = jnp.concatenate(
                    [jnp.where(lane_tile == k, group, 0.0) for k in range(gs)], axis=0
                ).astype(bf)
                g = h * (wh // DEPTH) + j
                near = f_v[0, g * gs:(g + 1) * gs].reshape(DEPTH, nq)
                blocks.append(dot(lhs, near).astype(bf))
        g_buf[mz, c] = jnp.concatenate(blocks, axis=0)

        for target in others:
            @pl.when(inner(target))
            def _(target=target, c=c):
                spread_to(target, mz, c).start()

    for side in range(2):
        @pl.when(helps[side])
        def _(side=side):
            tell(side, 0).wait_recv()
            tell(side, 1).wait_recv()
            li_end[side] = spread_links(l_end[side, 0], c_end[side])

    li[...] = spread_links(l_v[0], c_v[...])
    part_rows = tc * ROWS
    for i in range(nc):
        c = chunk_of(i)

        @pl.when(inner(mz))
        def _(c=c):
            for src in others:
                spread_to(src, src, c).wait_recv()

        for side in range(2):
            @pl.when(helps[side])
            def _(c=c, side=side):
                first, last = (0, nz - 1) if side else (1, nz)
                near = g_buf[first:last, c].reshape((last - first) * part_rows, nq)
                cols = li_end[side, :, first * part_rows:last * part_rows]
                p_out[side, c] = dot(cols, near).astype(bf)
                sum_hop(c, side).start()

        for side in range(2):
            @pl.when(is_end[side])
            def _(c=c, side=side):
                own = (nz - 1) * side
                mine = dot(li[:, own * part_rows:(own + 1) * part_rows], g_buf[own, c])
                sum_hop(c, side).wait_recv()
                tot[...] = mine + p_in[c].astype(f32)

        @pl.when(inner(mz))
        def _(c=c):
            tot[...] = dot(li[...], g_buf[:, c].reshape(gt * ROWS, nq))

        total = tot[...].astype(bf)
        flat = []
        for g in range(ng):
            near = f_v[0, g * gs:(g + 1) * gs].reshape(DEPTH, nq)
            mine = total[g * gs * ROWS:(g + 1) * gs * ROWS]
            crossed = lax.dot_general(
                mine, near, (((1,), (1,)), ((), ())), preferred_element_type=f32
            )
            kept = crossed[:ROWS]
            for k in range(1, gs):
                kept = jnp.where(lane_tile == k, crossed[k * ROWS:(k + 1) * ROWS], kept)
            flat.append(kept)
        flat = jnp.concatenate(flat, axis=1)
        halves = [flat[:, h * wh:(h + 1) * wh] for h in range(parts)]
        for d in range(parts):
            dev = c * parts + d
            slab = rows_of([shifted(halves[h], (h - d) * pd) for h in range(parts)])
            stage2[dev] = slab.astype(bf)

            @pl.when(dev != me)
            def _(dev=dev):
                swap(stage2, recv2, s2, r2, dev, me).start()

            @pl.when(dev == me)
            def _(dev=dev):
                recv2[dev] = stage2[dev]

    for rel in range(1, np_):
        peer = lax.rem(me + rel, np_)
        swap(stage2, recv2, s2, r2, peer, peer).wait_recv()
    landed = recv2[...].astype(f32).reshape(nb * ROWS, wh).astype(bf)
    shape = (pd * nb, nb * ROWS)
    row, col = iota(shape, 0), iota(shape, 1)
    for h in range(parts):
        back = ones_where(
            ((col & (ROWS - 1)) - h * pd) * nb + lax.shift_right_logical(col, 3) == row
        )
        o_ref[:, :, h * wh:(h + 1) * wh] = dot(back, landed).reshape(pd, nb, wh).astype(bf)

    for rel in range(1, np_):
        peer = lax.rem(me + rel, np_)
        swap(stage1, recv1, s1, r1, peer, me).wait_send()
        swap(stage2, recv2, s2, r2, peer, me).wait_send()
    for side in range(2):
        @pl.when(is_end[side])
        def _(side=side):
            tell(side, 0).wait_send()
            tell(side, 1).wait_send()

    for i in range(nc):
        for target in others:
            @pl.when(inner(target))
            def _(target=target, i=i):
                spread_to(target, mz, chunk_of(i)).wait_send()

        for side in range(2):
            @pl.when(helps[side])
            def _(i=i, side=side):
                sum_hop(chunk_of(i), side).wait_send()


def solution(mesh):
    np_, nz = mesh.shape["pair"], mesh.shape["ints"]

    def body(t_amps, block_mask, factors, links, link_counts):
        pd, nb, width = t_amps.shape
        _, tc, tile, nq = factors.shape
        parts = ROWS // pd
        nc = np_ * pd // ROWS
        slabs = (nb, ROWS, width // parts)
        bf = jnp.bfloat16
        return pl.pallas_call(
            functools.partial(kernel, np_, nz),
            out_shape=pltpu.VMEM(t_amps.shape, bf),
            in_specs=[pl.BlockSpec(memory_space=pl.ANY)] * 5,
            out_specs=pl.BlockSpec(memory_space=pltpu.VMEM),
            scratch_shapes=[
                pltpu.VMEM(t_amps.shape, bf),
                pltpu.VMEM(block_mask.shape, jnp.int32),
                pltpu.VMEM(factors.shape, bf),
                pltpu.VMEM(links.shape, jnp.int32),
                pltpu.VMEM(link_counts.shape, jnp.int32),
                pltpu.VMEM(slabs, bf),
                pltpu.VMEM(slabs, bf),
                pltpu.VMEM((nz, nc, tc * ROWS, nq), bf),
                pltpu.VMEM((tc * ROWS, nz * tc * ROWS), bf),
                pltpu.VMEM(slabs, bf),
                pltpu.VMEM(slabs, bf),
                pltpu.VMEM((2,) + links.shape, jnp.int32),
                pltpu.VMEM((2,) + link_counts.shape, jnp.int32),
                pltpu.VMEM((2, tc * ROWS, nz * tc * ROWS), bf),
                pltpu.VMEM((2, nc, tc * ROWS, nq), bf),
                pltpu.VMEM((nc, tc * ROWS, nq), bf),
                pltpu.VMEM((tc * ROWS, nq), jnp.float32),
                pltpu.SemaphoreType.DMA((5,)),
                pltpu.SemaphoreType.DMA((np_,)),
                pltpu.SemaphoreType.DMA((np_,)),
                pltpu.SemaphoreType.DMA((nz, nc)),
                pltpu.SemaphoreType.DMA((nz, nc)),
                pltpu.SemaphoreType.DMA((np_,)),
                pltpu.SemaphoreType.DMA((np_,)),
                pltpu.SemaphoreType.DMA((2, 2)),
                pltpu.SemaphoreType.DMA((2, 2)),
                pltpu.SemaphoreType.DMA((2, nc)),
                pltpu.SemaphoreType.DMA((nc,)),
            ],
            compiler_params=pltpu.CompilerParams(collective_id=0, has_side_effects=True),
        )(t_amps, block_mask, factors, links, link_counts)

    placed = (
        P("pair", None, "ints"),
        P("pair", None, "ints"),
        P("pair", "ints", None, None),
        P("pair", "ints", None),
        P("pair", "ints"),
    )
    return jax.shard_map(
        body, mesh=mesh, in_specs=placed, out_specs=P("pair", None, "ints"), check_vma=False
    )
```
